256 devices in a mesh: row: 32 (over x, y, core), col: 8 (over z).
Axes of the slice: x: 4, y: 4, z: 8, core: 2. Of those that a mesh axis runs over, the one named last changes fastest.
Arguments:
- kernel: float32 [4, 4096, 16, 1024], P(None, 'row', None, 'col'), as said below
Outputs:
- factored: float32 [4, 4096, 16, 1024], P(None, 'row', None, 'col')
Inputs may be any that keep to these rules, and one draw needn't show every extreme that they name: kernel is symmetric and positive definite.
All inputs are finite; a program needn't handle non-finite values.
Results may differ from the reference program's by a relative error of at most 0.0001.
Values sent between devices are 32-bit elements; how exact they have to be, the bound alone decides.
A program may use at most 128 MiB of HBM per device.

```python
import jax
import jax.numpy as jnp
from jax import lax

BS = 128
PANELS = 2
LR = 4
ROWSPAN = 4096
COLSPAN = 1024
LC = 16
M = 16384


def draw_kernel(key, part):
    breadth = 4 * BS
    key_factors = jax.random.fold_in(key, 21)
    key_nugget = jax.random.fold_in(key, 23)
    factors = jax.random.normal(key_factors, (M, breadth), jnp.float32)
    gram = jnp.dot(factors, factors.T, precision=lax.Precision.HIGHEST) * (1.0 / breadth)
    gram = (gram + gram.T) * 0.5
    nugget = jax.random.uniform(key_nugget, (M,), jnp.float32, 0.4, 0.8)
    indices = jnp.arange(M)
    eye_mask = indices[:, None] == indices[None, :]
    values = gram + jnp.where(eye_mask, nugget[:, None] * jnp.ones((1, M), jnp.float32), jnp.float32(0.0))
    return values.reshape(LR, ROWSPAN, LC, COLSPAN)


def setup_inputs(seed: int = 0) -> dict:
    splits = jax.random.split(jax.random.key(seed), 2)
    return {
        "kernel": draw_kernel(jax.random.fold_in(splits[1], 71), 0),
    }


def reference(kernel):
    matrix = kernel.reshape(M, M)
    row_ids = jnp.arange(M, dtype=jnp.int32)
    for panel_idx in range(PANELS):
        start = panel_idx * BS
        finish = start + BS
        factor = jnp.linalg.cholesky(matrix[start:finish, start:finish])
        column = matrix[:, start:finish]
        solved = jax.scipy.linalg.solve_triangular(factor, column.T, lower=True).T
        solved = jnp.where((row_ids < start)[:, None], jnp.float32(0.0), solved)
        solved = solved.at[start:finish].set(factor)
        matrix = matrix - jnp.dot(solved, solved.T, precision=lax.Precision.HIGHEST)
        matrix = matrix.at[:, start:finish].set(solved)
        matrix = matrix.at[start:finish, finish:].set(jnp.float32(0.0))
    return matrix.reshape(LR, ROWSPAN, LC, COLSPAN)
```

```python
import jax
import jax.numpy as jnp
from jax import lax
from jax.experimental import pallas as pl
from jax.experimental.pallas import tpu as pltpu
from jax.sharding import PartitionSpec as P

NX, NY, NZ = 4, 4, 8
BS = 128
GROUP = 8
GROUPS = BS // GROUP
QUARTERS = 4
PIECES = 4
MESH = pl.DeviceIdType.MESH


def dot_nn(a, b):
    return lax.dot_general(
        a,
        b,
        (((1,), (0,)), ((), ())),
        precision=lax.Precision.HIGHEST,
        preferred_element_type=jnp.float32,
    )


def dot_nt(a, b):
    return lax.dot_general(
        a,
        b,
        (((1,), (1,)), ((), ())),
        precision=lax.Precision.HIGHEST,
        preferred_element_type=jnp.float32,
    )


def lane(value, index):
    return jnp.broadcast_to(value[:, index : index + 1], (GROUP, BS))


def factor_block(block, upper_ref, inverse_ref, hook):
    rows = lax.broadcasted_iota(jnp.int32, (GROUP, BS), 0)
    cols = lax.broadcasted_iota(jnp.int32, (GROUP, BS), 1)
    left = [block[GROUP * g : GROUP * (g + 1), :] for g in range(GROUPS)]
    right = [jnp.where(cols == rows + GROUP * g, 1.0, 0.0).astype(jnp.float32) for g in range(GROUPS)]
    for k in range(GROUPS):
        hook(k)
        base = GROUP * k
        r = [jnp.broadcast_to(left[k][i : i + 1, :], (GROUP, BS)) for i in range(GROUP)]
        q = [jnp.broadcast_to(right[k][i : i + 1, :], (GROUP, BS)) for i in range(GROUP)]
        d = [[lane(r[i], base + j) if j <= i else None for j in range(GROUP)] for i in range(GROUP)]
        c = [[lane(left[g], base + p) for p in range(GROUP)] for g in range(k + 1, GROUPS)]
        inv = [None] * GROUP
        for p in range(GROUP):
            inv[p] = lax.rsqrt(d[p][p])
            for i in range(p + 1, GROUP):
                d[i][p] = d[i][p] * inv[p]
            r[p] = r[p] * inv[p]
            q[p] = q[p] * inv[p]
            for i in range(p + 1, GROUP):
                for j in range(p + 1, i + 1):
                    d[i][j] = d[i][j] - d[i][p] * d[j][p]
                r[i] = r[i] - d[i][p] * r[p]
                q[i] = q[i] - d[i][p] * q[p]
            if k + 1 < GROUPS:
                first = c[0]
                first[p] = first[p] * inv[p]
                for j in range(p + 1, GROUP):
                    first[j] = first[j] - first[p] * d[j][p]
                left[k + 1] = left[k + 1] - first[p] * r[p]
                right[k + 1] = right[k + 1] - first[p] * q[p]
        for p in range(GROUP):
            at = base + p
            upper_ref[at : at + 1, :] = jnp.where(cols[0:1] >= at, r[p][0:1], 0.0)
            inverse_ref[at : at + 1, :] = q[p][0:1]
        if k + 2 < GROUPS:
            v = [None] * GROUP
            w = [None] * GROUP
            for p in range(GROUP - 1, -1, -1):
                a, b = r[p], q[p]
                for s in range(p + 1, GROUP):
                    a = a - d[s][p] * v[s]
                    b = b - d[s][p] * w[s]
                v[p] = a * inv[p]
                w[p] = b * inv[p]
            for g in range(k + 2, GROUPS):
                mult = c[g - k - 1]
                for p in range(GROUP):
                    left[g] = left[g] - mult[p] * v[p]
                    right[g] = right[g] - mult[p] * w[p]


def remote(src, dst, send, recv, target):
    return pltpu.make_async_remote_copy(
        src_ref=src, dst_ref=dst, send_sem=send, recv_sem=recv, device_id=target, device_id_type=MESH
    )


def panels_kernel(
    a_ref,
    pr_ref,
    pc_ref,
    cbuf,
    rbuf,
    corner,
    upper,
    inverse,
    load_c,
    load_r,
    r_send,
    r_recv,
    k_send,
    k_recv,
    c_send,
    c_recv,
):
    grid_row = lax.axis_index("row")
    z = lax.axis_index("col")
    core = lax.rem(grid_row, 2)
    y = lax.rem(grid_row // 2, NY)
    x = grid_row // (2 * NY)

    def at(i, j, core_, z_):
        return ((lax.rem(i, NX) * NY + lax.rem(j, NY)) * 2 + core_, lax.rem(z_, NZ))

    sibling = at(x, y, 1 - core, z)
    root = (x == 0) & (y == 0)
    mine = pl.multiple_of(core * BS, BS)

    def c_load(j):
        return pltpu.make_async_copy(
            a_ref.at[0, :, j, :], cbuf.at[pl.ds(mine, BS), pl.ds(j * BS, BS)], load_c.at[j]
        )

    def r_load(panel, i):
        return pltpu.make_async_copy(a_ref.at[i, :, 0, :], rbuf.at[panel, i], load_r.at[i])

    for panel in range(2):

        @pl.when(z == panel)
        def _():
            for i in range(4):
                r_load(panel, i).start()

    @pl.when(root)
    def _():
        for j in range(16):
            c_load(j).start()

    barrier = pltpu.get_barrier_semaphore()
    near = [at(x + m, y, core, z) for m in range(1, NX)]
    near += [at(x, y + m, core, z) for m in range(1, NY)]
    near += [at(x, y, core, z + 1), at(x, y, core, z + NZ - 1), sibling]
    for target in near:
        pl.semaphore_signal(barrier, inc=1, device_id=target, device_id_type=MESH)
    pl.semaphore_wait(barrier, len(near))

    def r_copy(panel, i, up):
        step = 1 if up else NZ - 1
        return remote(
            rbuf.at[panel, i],
            rbuf.at[panel, i],
            r_send.at[panel, i, 0 if up else 1],
            r_recv.at[panel, i],
            at(x, y, core, z + step),
        )

    def r_where(panel):
        rel = lax.rem(z + NZ - panel, NZ)
        return rel == 0, rel <= 3, (rel == 0) | (rel >= 6)

    def r_relay(panel, i):
        first, up, down = r_where(panel)

        @pl.when(first)
        def _():
            r_load(panel, i).wait()

        @pl.when(jnp.logical_not(first))
        def _():
            r_copy(panel, i, True).wait_recv()

        @pl.when(up)
        def _():
            r_copy(panel, i, True).start()

        @pl.when(down)
        def _():
            r_copy(panel, i, False).start()

    def r_finish(panel, i):
        _, up, down = r_where(panel)

        @pl.when(up)
        def _():
            r_copy(panel, i, True).wait_send()

        @pl.when(down)
        def _():
            r_copy(panel, i, False).wait_send()

    owners = (0, 1, 1)
    sources = ((0, 0), (0, 0), (1, 0))

    def k_copy(block, slot, target):
        return remote(corner.at[block], corner.at[block], k_send.at[block, slot], k_recv.at[block], target)

    def k_relay(block):
        owner = core == owners[block]

        @pl.when(owner & root)
        def _():
            corner[block] = rbuf[sources[block]]
            for m in range(1, NX):
                k_copy(block, m - 1, at(x + m, y, core, z)).start()

        @pl.when(jnp.logical_not(owner & root))
        def _():
            k_copy(block, 0, sibling).wait_recv()

        @pl.when(owner & (y == 0))
        def _():
            for m in range(1, NY):
                k_copy(block, NX - 2 + m, at(x, y + m, core, z)).start()

        @pl.when(owner)
        def _():
            k_copy(block, NX + NY - 2, sibling).start()

    def k_finish(block):
        owner = core == owners[block]

        @pl.when(owner & root)
        def _():
            for m in range(1, NX):
                k_copy(block, m - 1, at(x + m, y, core, z)).wait_send()

        @pl.when(owner & (y == 0))
        def _():
            for m in range(1, NY):
                k_copy(block, NX - 2 + m, at(x, y + m, core, z)).wait_send()

        @pl.when(owner)
        def _():
            k_copy(block, NX + NY - 2, sibling).wait_send()

    def c_where(quarter):
        flip = quarter % 2
        a, b = (x, y) if quarter < 2 else (y, x)
        if flip:
            a, b = lax.rem(NX - a, NX), lax.rem(NY - b, NY)
        step = NX - 1 if flip else 1
        along, across = ((step, 0), (0, step)) if quarter < 2 else ((0, step), (step, 0))
        send_along = ((b == 0) & (a < 3)) | ((b > 0) & (a == 3))
        send_across = (a > 0) & (b < 3)
        return (
            send_along,
            at(x + along[0], y + along[1], core, z),
            send_across,
            at(x + across[0], y + across[1], core, z),
        )

    def c_rows(quarter, piece, base):
        height = BS // QUARTERS // PIECES
        return pl.ds(pl.multiple_of(base + (quarter * PIECES + piece) * height, height), height)

    def c_copy(quarter, piece, slot, target):
        view = cbuf.at[c_rows(quarter, piece, mine)]
        return remote(view, view, c_send.at[quarter, piece, slot], c_recv.at[quarter, piece, 0], target)

    def c_pair(quarter, piece):
        view = cbuf.at[c_rows(quarter, piece, mine)]
        return remote(view, view, c_send.at[quarter, piece, 2], c_recv.at[quarter, piece, 1], sibling)

    def c_pair_in(quarter, piece):
        view = cbuf.at[c_rows(quarter, piece, BS - mine)]
        return remote(view, view, c_send.at[quarter, piece, 2], c_recv.at[quarter, piece, 1], sibling)

    def c_relay(quarter, piece):
        send_along, along, send_across, across = c_where(quarter)

        @pl.when(jnp.logical_not(root))
        def _():
            c_copy(quarter, piece, 0, sibling).wait_recv()

        @pl.when(send_along)
        def _():
            c_copy(quarter, piece, 0, along).start()

        @pl.when(send_across)
        def _():
            c_copy(quarter, piece, 1, across).start()

        c_pair(quarter, piece).start()

    def c_finish(quarter, piece):
        send_along, along, send_across, across = c_where(quarter)

        @pl.when(send_along)
        def _():
            c_copy(quarter, piece, 0, along).wait_send()

        @pl.when(send_across)
        def _():
            c_copy(quarter, piece, 1, across).wait_send()

        c_pair(quarter, piece).wait_send()

    r_relay(0, 0)
    k_relay(0)
    r_relay(1, 0)
    k_relay(1)
    k_relay(2)

    @pl.when(root)
    def _():
        for j in range(16):
            c_load(j).wait()

    events = []
    for piece in range(PIECES):
        for quarter in range(QUARTERS):
            events.append((c_relay, quarter, piece))
        if piece < 3:
            events.append((r_relay, 0, piece + 1))
            events.append((r_relay, 1, piece + 1))
    pending = list(events)

    def run(count):
        for _ in range(count):
            if pending:
                f, i, j = pending.pop(0)
                f(i, j)

    factor_block(corner[0], upper.at[0], inverse.at[0], lambda k: run(1))
    below = dot_nt(corner[1], inverse[0])
    second = corner[2] - dot_nt(below, below)
    factor_block(second, upper.at[1], inverse.at[1], lambda k: run(1))
    run(len(pending))

    for i in range(4):
        first_rows = dot_nt(rbuf[0, i], inverse[0])
        pr_ref[i, :, 0:BS] = first_rows
        pr_ref[i, :, BS : 2 * BS] = dot_nt(rbuf[1, i] - dot_nt(first_rows, below), inverse[1])

    @pl.when(grid_row == 0)
    def _():
        pr_ref[0, :, 0:BS] = upper[0].T
        pr_ref[0, :, BS : 2 * BS] = jnp.zeros((BS, BS), jnp.float32)

    @pl.when(grid_row == 1)
    def _():
        pr_ref[0, :, BS : 2 * BS] = upper[1].T

    for quarter in range(QUARTERS):
        for piece in range(PIECES):
            c_pair_in(quarter, piece).wait_recv()
    for j in range(4):
        part = pl.ds(j * 512, 512)
        top = dot_nn(inverse[0], cbuf[0:BS, part])
        pc_ref[0:BS, part] = top
        pc_ref[BS : 2 * BS, part] = dot_nn(inverse[1], cbuf[BS : 2 * BS, part] - dot_nn(below, top))

    for i in range(4):
        for panel in range(2):
            r_finish(panel, i)
    for block in range(3):
        k_finish(block)
    for quarter in range(QUARTERS):
        for piece in range(PIECES):
            c_finish(quarter, piece)


def update_kernel(a_ref, pr_ref, pc_ref, out_ref):
    step = pl.program_id(0)
    grid_row = lax.axis_index("row")
    z = lax.axis_index("col")
    top = (step == 0) & (grid_row < 2)

    @pl.when(top)
    def _():
        out_ref[...] = jnp.zeros_like(out_ref)

    @pl.when(jnp.logical_not(top))
    def _():
        for j in range(16):
            out_ref[0, :, j, :] = a_ref[0, :, j, :] - dot_nn(pr_ref[0], pc_ref[:, j * BS : (j + 1) * BS])

    @pl.when(z == 0)
    def _():
        out_ref[0, :, 0, :] = pr_ref[0, :, 0:BS]

    @pl.when(z == 1)
    def _():
        out_ref[0, :, 0, :] = pr_ref[0, :, BS : 2 * BS]


def shards(kernel):
    f32 = jnp.float32
    pr, pc = pl.pallas_call(
        panels_kernel,
        out_shape=[jax.ShapeDtypeStruct((4, BS, 2 * BS), f32), jax.ShapeDtypeStruct((2 * BS, 16 * BS), f32)],
        in_specs=[pl.BlockSpec(memory_space=pl.ANY)],
        out_specs=[pl.BlockSpec(memory_space=pltpu.VMEM)] * 2,
        scratch_shapes=[
            pltpu.VMEM((2 * BS, 16 * BS), f32),
            pltpu.VMEM((2, 4, BS, BS), f32),
            pltpu.VMEM((3, BS, BS), f32),
            pltpu.VMEM((2, BS, BS), f32),
            pltpu.VMEM((2, BS, BS), f32),
            pltpu.SemaphoreType.DMA((16,)),
            pltpu.SemaphoreType.DMA((4,)),
            pltpu.SemaphoreType.DMA((2, 4, 2)),
            pltpu.SemaphoreType.DMA((2, 4)),
            pltpu.SemaphoreType.DMA((3, NX + NY - 1)),
            pltpu.SemaphoreType.DMA((3,)),
            pltpu.SemaphoreType.DMA((QUARTERS, PIECES, 3)),
            pltpu.SemaphoreType.DMA((QUARTERS, PIECES, 2)),
        ],
        compiler_params=pltpu.CompilerParams(
            collective_id=0, has_side_effects=True, vmem_limit_bytes=24 * 1024 * 1024
        ),
        name="panels",
    )(kernel)
    return pl.pallas_call(
        update_kernel,
        grid=(4,),
        out_shape=jax.ShapeDtypeStruct(kernel.shape, f32),
        in_specs=[
            pl.BlockSpec((1, BS, 16, BS), lambda i: (i, 0, 0, 0)),
            pl.BlockSpec((1, BS, 2 * BS), lambda i: (i, 0, 0)),
            pl.BlockSpec((2 * BS, 16 * BS), lambda i: (0, 0)),
        ],
        out_specs=pl.BlockSpec((1, BS, 16, BS), lambda i: (i, 0, 0, 0)),
        compiler_params=pltpu.CompilerParams(vmem_limit_bytes=32 * 1024 * 1024),
        name="update",
    )(kernel, pr, pc)


def solution(mesh):
    spec = P(None, "row", None, "col")
    return jax.shard_map(shards, mesh=mesh, in_specs=(spec,), out_specs=spec, check_vma=False)
```

```python
import jax
import jax.numpy as jnp
from jax import lax
from jax.experimental import pallas as pl
from jax.experimental.pallas import tpu as pltpu
from jax.sharding import PartitionSpec as P

NX, NY, NZ = 4, 4, 8
BS = 128
GROUP = 8
GROUPS = BS // GROUP
QUARTERS = 4
PIECES = 4
MESH = pl.DeviceIdType.MESH


def dot_nn(a, b):
    return lax.dot_general(
        a,
        b,
        (((1,), (0,)), ((), ())),
        precision=lax.Precision.HIGHEST,
        preferred_element_type=jnp.float32,
    )


def dot_nt(a, b):
    return lax.dot_general(
        a,
        b,
        (((1,), (1,)), ((), ())),
        precision=lax.Precision.HIGHEST,
        preferred_element_type=jnp.float32,
    )


def split(value):
    high = value.astype(jnp.bfloat16)
    return high, (value - high.astype(jnp.float32)).astype(jnp.bfloat16)


def dot3(a, b, over):
    def one(p, q):
        return lax.dot_general(p, q, (((1,), (over,)), ((), ())), preferred_element_type=jnp.float32)

    return one(a[0], b[0]) + (one(a[1], b[0]) + one(a[0], b[1]))


def lane(value, index):
    return jnp.broadcast_to(value[:, index : index + 1], (GROUP, BS))


def factor_block(block, upper_ref, inverse_ref, hook):
    rows = lax.broadcasted_iota(jnp.int32, (GROUP, BS), 0)
    cols = lax.broadcasted_iota(jnp.int32, (GROUP, BS), 1)
    left = [block[GROUP * g : GROUP * (g + 1), :] for g in range(GROUPS)]
    right = [jnp.where(cols == rows + GROUP * g, 1.0, 0.0).astype(jnp.float32) for g in range(GROUPS)]
    for k in range(GROUPS):
        hook(k)
        base = GROUP * k
        r = [jnp.broadcast_to(left[k][i : i + 1, :], (GROUP, BS)) for i in range(GROUP)]
        q = [jnp.broadcast_to(right[k][i : i + 1, :], (GROUP, BS)) for i in range(GROUP)]
        d = [[lane(r[i], base + j) if j <= i else None for j in range(GROUP)] for i in range(GROUP)]
        c = [[lane(left[g], base + p) for p in range(GROUP)] for g in range(k + 1, GROUPS)]
        inv = [None] * GROUP
        for p in range(GROUP):
            inv[p] = lax.rsqrt(d[p][p])
            for i in range(p + 1, GROUP):
                d[i][p] = d[i][p] * inv[p]
            r[p] = r[p] * inv[p]
            q[p] = q[p] * inv[p]
            for i in range(p + 1, GROUP):
                for j in range(p + 1, i + 1):
                    d[i][j] = d[i][j] - d[i][p] * d[j][p]
                r[i] = r[i] - d[i][p] * r[p]
                q[i] = q[i] - d[i][p] * q[p]
            if k + 1 < GROUPS:
                first = c[0]
                first[p] = first[p] * inv[p]
                for j in range(p + 1, GROUP):
                    first[j] = first[j] - first[p] * d[j][p]
                left[k + 1] = left[k + 1] - first[p] * r[p]
                right[k + 1] = right[k + 1] - first[p] * q[p]
        for p in range(GROUP):
            at = base + p
            upper_ref[at : at + 1, :] = jnp.where(cols[0:1] >= at, r[p][0:1], 0.0)
            inverse_ref[at : at + 1, :] = q[p][0:1]
        if k + 2 < GROUPS:
            v = [None] * GROUP
            w = [None] * GROUP
            for p in range(GROUP - 1, -1, -1):
                a, b = r[p], q[p]
                for s in range(p + 1, GROUP):
                    a = a - d[s][p] * v[s]
                    b = b - d[s][p] * w[s]
                v[p] = a * inv[p]
                w[p] = b * inv[p]
            for g in range(k + 2, GROUPS):
                mult = c[g - k - 1]
                for p in range(GROUP):
                    left[g] = left[g] - mult[p] * v[p]
                    right[g] = right[g] - mult[p] * w[p]


def remote(src, dst, send, recv, target):
    return pltpu.make_async_remote_copy(
        src_ref=src, dst_ref=dst, send_sem=send, recv_sem=recv, device_id=target, device_id_type=MESH
    )


def panels_kernel(
    a_ref,
    pr_high,
    pr_low,
    pc_high,
    pc_low,
    own,
    flat,
    cbuf,
    rbuf,
    corner,
    upper,
    inverse,
    load_c,
    load_r,
    load_a,
    r_send,
    r_recv,
    k_send,
    k_recv,
    c_send,
    c_recv,
):
    grid_row = lax.axis_index("row")
    z = lax.axis_index("col")
    core = lax.rem(grid_row, 2)
    y = lax.rem(grid_row // 2, NY)
    x = grid_row // (2 * NY)

    def at(i, j, core_, z_):
        return ((lax.rem(i, NX) * NY + lax.rem(j, NY)) * 2 + core_, lax.rem(z_, NZ))

    sibling = at(x, y, 1 - core, z)
    root = (x == 0) & (y == 0)
    mine = pl.multiple_of(core * BS, BS)

    barrier = pltpu.get_barrier_semaphore()
    near = [at(x + m, y, core, z) for m in range(1, NX)]
    near += [at(x, y + m, core, z) for m in range(1, NY)]
    near += [at(x, y, core, z + m) for m in range(1, NZ)] + [sibling]
    for target in near:
        pl.semaphore_signal(barrier, inc=1, device_id=target, device_id_type=MESH)

    def c_load(j):
        return pltpu.make_async_copy(
            a_ref.at[0, :, j, :], cbuf.at[pl.ds(mine, BS), pl.ds(j * BS, BS)], load_c.at[j]
        )

    def r_load(panel, i):
        return pltpu.make_async_copy(a_ref.at[i, :, 0, :], rbuf.at[panel, i], load_r.at[i])

    def a_load(i, j):
        return pltpu.make_async_copy(a_ref.at[i, :, j, :], flat.at[i, :, pl.ds(j * BS, BS)], load_a.at[i, j])

    for panel in range(2):

        @pl.when(z == panel)
        def _():
            for i in range(4):
                r_load(panel, i).start()

    @pl.when(root)
    def _():
        for j in range(16):
            c_load(j).start()

    for panel in range(2):

        @pl.when(z == panel)
        def _():
            for i in range(4):
                r_load(panel, i).wait()

    @pl.when(root)
    def _():
        for j in range(16):
            c_load(j).wait()

    for i in range(4):
        for j in range(16):
            a_load(i, j).start()

    pl.semaphore_wait(barrier, len(near))

    def r_where(panel):
        rel = lax.rem(z + NZ - panel, NZ)
        return rel == 0, rel <= 3, (rel == 0) | (rel >= 6), jnp.where(rel <= 4, rel, NZ - rel)

    def r_copy(panel, i, up):
        step = 1 if up else NZ - 1
        return remote(
            rbuf.at[panel, i],
            rbuf.at[panel, i],
            r_send.at[panel, i, 0 if up else 1],
            r_recv.at[panel, i],
            at(x, y, core, z + step),
        )

    def r_relay(slot):
        for panel in range(2):
            first, up, down, depth = r_where(panel)
            i = slot - depth
            live = (i >= 0) & (i < 4)

            @pl.when(live & jnp.logical_not(first))
            def _():
                r_copy(panel, i, True).wait_recv()

            @pl.when(live & up)
            def _():
                r_copy(panel, i, True).start()

            @pl.when(live & down)
            def _():
                r_copy(panel, i, False).start()

    def r_finish(panel, i):
        _, up, down, _ = r_where(panel)

        @pl.when(up)
        def _():
            r_copy(panel, i, True).wait_send()

        @pl.when(down)
        def _():
            r_copy(panel, i, False).wait_send()

    owners = (0, 1, 1)
    planes = (0, 0, 1)

    def k_copy(block, slot, target):
        return remote(corner.at[block], corner.at[block], k_send.at[block, slot], k_recv.at[block], target)

    def k_sends(block):
        owner = core == owners[block]
        source = owner & root & (z == planes[block])
        stages = [(source, [k_copy(block, m - 1, at(x, y, core, z + m)) for m in range(1, NZ)])]
        stages.append((owner & root, [k_copy(block, 6 + m, at(x + m, y, core, z)) for m in range(1, NX)]))
        stages.append((owner & (y == 0), [k_copy(block, 9 + m, at(x, y + m, core, z)) for m in range(1, NY)]))
        stages.append((owner, [k_copy(block, 13, sibling)]))
        return source, stages

    def k_relay(block):
        source, stages = k_sends(block)

        @pl.when(source)
        def _():
            corner[block] = rbuf[planes[block], 0]

        @pl.when(jnp.logical_not(source))
        def _():
            k_copy(block, 0, sibling).wait_recv()

        for cond, copies in stages:

            @pl.when(cond)
            def _(copies=copies):
                for copy in copies:
                    copy.start()

    def k_finish(block):
        for cond, copies in k_sends(block)[1]:

            @pl.when(cond)
            def _(copies=copies):
                for copy in copies:
                    copy.wait_send()

    def c_where(quarter):
        flip = quarter % 2
        a, b = (x, y) if quarter < 2 else (y, x)
        if flip:
            a, b = lax.rem(NX - a, NX), lax.rem(NY - b, NY)
        step = NX - 1 if flip else 1
        along, across = ((step, 0), (0, step)) if quarter < 2 else ((0, step), (step, 0))
        send_along = ((b == 0) & (a < 3)) | ((b > 0) & (a == 3))
        send_across = (a > 0) & (b < 3)
        depth = jnp.where((a == 0) & (b > 0), 4 + b, a + b)
        return (
            send_along,
            at(x + along[0], y + along[1], core, z),
            send_across,
            at(x + across[0], y + across[1], core, z),
            depth,
        )

    def c_rows(quarter, piece, base):
        height = BS // QUARTERS // PIECES
        return pl.ds(pl.multiple_of(base + (quarter * PIECES + piece) * height, height), height)

    def c_copy(quarter, piece, slot, target):
        view = cbuf.at[c_rows(quarter, piece, mine)]
        return remote(view, view, c_send.at[quarter, piece, slot], c_recv.at[quarter, piece, 0], target)

    def c_pair(quarter, piece):
        view = cbuf.at[c_rows(quarter, piece, mine)]
        return remote(view, view, c_send.at[quarter, piece, 2], c_recv.at[quarter, piece, 1], sibling)

    def c_pair_in(quarter, piece):
        view = cbuf.at[c_rows(quarter, piece, BS - mine)]
        return remote(view, view, c_send.at[quarter, piece, 2], c_recv.at[quarter, piece, 1], sibling)

    def c_relay(slot):
        for quarter in range(QUARTERS):
            send_along, along, send_across, across, depth = c_where(quarter)
            piece = slot - depth

            @pl.when((piece >= 0) & (piece < PIECES))
            def _():
                @pl.when(jnp.logical_not(root))
                def _():
                    c_copy(quarter, piece, 0, sibling).wait_recv()

                @pl.when(send_along)
                def _():
                    c_copy(quarter, piece, 0, along).start()

                @pl.when(send_across)
                def _():
                    c_copy(quarter, piece, 1, across).start()

                c_pair(quarter, piece).start()

    def c_finish(quarter, piece):
        send_along, along, send_across, across, _ = c_where(quarter)

        @pl.when(send_along)
        def _():
            c_copy(quarter, piece, 0, along).wait_send()

        @pl.when(send_across)
        def _():
            c_copy(quarter, piece, 1, across).wait_send()

        c_pair(quarter, piece).wait_send()

    k_relay(0)
    c_relay(0)
    r_relay(0)
    c_relay(1)
    r_relay(1)
    k_relay(1)
    k_relay(2)
    pending = []
    for slot in range(2, 7 + PIECES):
        pending.append((c_relay, slot))
        if slot < 8:
            pending.append((r_relay, slot))

    def run(count):
        for _ in range(count):
            if pending:
                f, slot = pending.pop(0)
                f(slot)

    factor_block(corner[0], upper.at[0], inverse.at[0], lambda k: run(1))
    below = dot_nt(corner[1], inverse[0])
    second = corner[2] - dot_nt(below, below)
    factor_block(second, upper.at[1], inverse.at[1], lambda k: run(1))
    run(len(pending))

    first_inverse, second_inverse, below_pair = split(inverse[0]), split(inverse[1]), split(below)

    def keep(i, panel, rows):
        part = slice(panel * BS, (panel + 1) * BS)
        high, low = split(rows)
        pr_high[i, :, part] = high
        pr_low[i, :, part] = low

        @pl.when(z == panel)
        def _():
            own[i] = rows

    for i in range(4):
        first_rows = dot3(split(rbuf[0, i]), first_inverse, 1)
        keep(i, 0, first_rows)
        rest = rbuf[1, i] - dot3(split(first_rows), below_pair, 1)
        keep(i, 1, dot3(split(rest), second_inverse, 1))

    @pl.when((grid_row == 0) & (z == 0))
    def _():
        own[0] = upper[0].T

    @pl.when((grid_row == 0) & (z == 1))
    def _():
        own[0] = jnp.zeros((BS, BS), jnp.float32)

    @pl.when((grid_row == 1) & (z == 1))
    def _():
        own[0] = upper[1].T

    for quarter in range(QUARTERS):
        for piece in range(PIECES):
            c_pair_in(quarter, piece).wait_recv()
    for j in range(4):
        part = pl.ds(j * 512, 512)
        top = split(dot3(first_inverse, split(cbuf[0:BS, part]), 0))
        pc_high[0:BS, part], pc_low[0:BS, part] = top
        rest = cbuf[BS : 2 * BS, part] - dot3(below_pair, top, 0)
        low_half = split(dot3(second_inverse, split(rest), 0))
        pc_high[BS : 2 * BS, part], pc_low[BS : 2 * BS, part] = low_half

    for i in range(4):
        for panel in range(2):
            r_finish(panel, i)
    for block in range(3):
        k_finish(block)
    for quarter in range(QUARTERS):
        for piece in range(PIECES):
            c_finish(quarter, piece)
    for i in range(4):
        for j in range(16):
            a_load(i, j).wait()


def update_kernel(flat, pr_high, pr_low, pc_high, pc_low, own, out_ref, tiles, store):
    grid_row = lax.axis_index("row")
    z = lax.axis_index("col")
    wide = 4

    def out_copy(i):
        return pltpu.make_async_copy(tiles.at[i], out_ref.at[i], store.at[i])

    for i in range(4):
        for j in range(0, 16, wide):
            part = slice(j * BS, (j + wide) * BS)
            rows = (pr_high[i], pr_low[i])
            new = flat[i, :, part] - dot3(rows, (pc_high[:, part], pc_low[:, part]), 0)
            for m in range(wide):
                tiles[i, :, j + m, :] = new[:, m * BS : (m + 1) * BS]
        if i == 0:

            @pl.when(grid_row < 2)
            def _():
                tiles[0] = jnp.zeros((BS, 16, BS), jnp.float32)

        @pl.when(z < 2)
        def _():
            tiles[i, :, 0, :] = own[i]

        out_copy(i).start()
    for i in range(4):
        out_copy(i).wait()


def shards(kernel):
    f32, bf16 = jnp.float32, jnp.bfloat16
    vmem = pl.BlockSpec(memory_space=pltpu.VMEM)
    *factors, flat = pl.pallas_call(
        panels_kernel,
        out_shape=[
            jax.ShapeDtypeStruct((4, BS, 2 * BS), bf16),
            jax.ShapeDtypeStruct((4, BS, 2 * BS), bf16),
            jax.ShapeDtypeStruct((2 * BS, 16 * BS), bf16),
            jax.ShapeDtypeStruct((2 * BS, 16 * BS), bf16),
            jax.ShapeDtypeStruct((4, BS, BS), f32),
            jax.ShapeDtypeStruct((4, BS, 16 * BS), f32),
        ],
        in_specs=[pl.BlockSpec(memory_space=pltpu.HBM)],
        out_specs=[vmem] * 6,
        scratch_shapes=[
            pltpu.VMEM((2 * BS, 16 * BS), f32),
            pltpu.VMEM((2, 4, BS, BS), f32),
            pltpu.VMEM((3, BS, BS), f32),
            pltpu.VMEM((2, BS, BS), f32),
            pltpu.VMEM((2, BS, BS), f32),
            pltpu.SemaphoreType.DMA((16,)),
            pltpu.SemaphoreType.DMA((4,)),
            pltpu.SemaphoreType.DMA((4, 16)),
            pltpu.SemaphoreType.DMA((2, 4, 2)),
            pltpu.SemaphoreType.DMA((2, 4)),
            pltpu.SemaphoreType.DMA((3, 14)),
            pltpu.SemaphoreType.DMA((3,)),
            pltpu.SemaphoreType.DMA((QUARTERS, PIECES, 3)),
            pltpu.SemaphoreType.DMA((QUARTERS, PIECES, 2)),
        ],
        compiler_params=pltpu.CompilerParams(
            collective_id=0, has_side_effects=True, vmem_limit_bytes=44 * 1024 * 1024
        ),
        name="panels",
    )(kernel)
    return pl.pallas_call(
        update_kernel,
        out_shape=jax.ShapeDtypeStruct(kernel.shape, f32),
        in_specs=[vmem] * 6,
        out_specs=pl.BlockSpec(memory_space=pltpu.HBM),
        scratch_shapes=[pltpu.VMEM((4, BS, 16, BS), f32), pltpu.SemaphoreType.DMA((4,))],
        compiler_params=pltpu.CompilerParams(vmem_limit_bytes=32 * 1024 * 1024),
        name="update",
    )(flat, *factors)


def solution(mesh):
    spec = P(None, "row", None, "col")
    return jax.shard_map(shards, mesh=mesh, in_specs=(spec,), out_specs=spec, check_vma=False)
```

```python
import jax
import jax.numpy as jnp
from jax import lax
from jax.experimental import pallas as pl
from jax.experimental.pallas import tpu as pltpu
from jax.sharding import PartitionSpec as P

NX, NY, NZ = 4, 4, 8
BS = 128
GROUP = 8
GROUPS = BS // GROUP
QUARTERS = 4
PIECES = 8
C_LAG = 4
STEPS = ((1, 0), (0, 1), (NX - 1, 0), (0, NY - 1))
CHILDREN = {
    (0, 0): (0,),
    (1, 0): (0, 1, 3),
    (2, 0): (3, 0),
    (1, 1): (1, 2, 0),
    (1, 3): (2,),
    (2, 1): (0,),
    (2, 3): (3, 0),
    (1, 2): (2,),
    (2, 2): (0,),
}


def tree_depths():
    depths = {(0, 0): 0}
    todo = [(0, 0)]
    while todo:
        a, b = todo.pop()
        for d in CHILDREN.get((a, b), ()):
            child = ((a + STEPS[d][0]) % NX, (b + STEPS[d][1]) % NY)
            depths[child] = depths[(a, b)] + 1
            todo.append(child)
    return depths


DEPTHS = tree_depths()
assert len(DEPTHS) == NX * NY
DEEPEST = max(DEPTHS.values())
MESH = pl.DeviceIdType.MESH


def dot_nn(a, b):
    return lax.dot_general(
        a,
        b,
        (((1,), (0,)), ((), ())),
        precision=lax.Precision.HIGHEST,
        preferred_element_type=jnp.float32,
    )


def dot_nt(a, b):
    return lax.dot_general(
        a,
        b,
        (((1,), (1,)), ((), ())),
        precision=lax.Precision.HIGHEST,
        preferred_element_type=jnp.float32,
    )


def split(value):
    high = value.astype(jnp.bfloat16)
    return high, (value - high.astype(jnp.float32)).astype(jnp.bfloat16)


def dot3(a, b, over):
    def one(p, q):
        return lax.dot_general(p, q, (((1,), (over,)), ((), ())), preferred_element_type=jnp.float32)

    return one(a[0], b[0]) + (one(a[1], b[0]) + one(a[0], b[1]))


def lane(value, index):
    return jnp.broadcast_to(value[:, index : index + 1], (GROUP, BS))


def factor_block(block, upper_ref, inverse_ref, hook):
    rows = lax.broadcasted_iota(jnp.int32, (GROUP, BS), 0)
    cols = lax.broadcasted_iota(jnp.int32, (GROUP, BS), 1)
    left = [block[GROUP * g : GROUP * (g + 1), :] for g in range(GROUPS)]
    right = [jnp.where(cols == rows + GROUP * g, 1.0, 0.0).astype(jnp.float32) for g in range(GROUPS)]
    for k in range(GROUPS):
        hook(k)
        base = GROUP * k
        r = [jnp.broadcast_to(left[k][i : i + 1, :], (GROUP, BS)) for i in range(GROUP)]
        q = [jnp.broadcast_to(right[k][i : i + 1, :], (GROUP, BS)) for i in range(GROUP)]
        d = [[lane(r[i], base + j) if j <= i else None for j in range(GROUP)] for i in range(GROUP)]
        c = [[lane(left[g], base + p) for p in range(GROUP)] for g in range(k + 1, GROUPS)]
        inv = [None] * GROUP
        for p in range(GROUP):
            inv[p] = lax.rsqrt(d[p][p])
            for i in range(p + 1, GROUP):
                d[i][p] = d[i][p] * inv[p]
            r[p] = r[p] * inv[p]
            q[p] = q[p] * inv[p]
            for i in range(p + 1, GROUP):
                for j in range(p + 1, i + 1):
                    d[i][j] = d[i][j] - d[i][p] * d[j][p]
                r[i] = r[i] - d[i][p] * r[p]
                q[i] = q[i] - d[i][p] * q[p]
            if k + 1 < GROUPS:
                first = c[0]
                first[p] = first[p] * inv[p]
                for j in range(p + 1, GROUP):
                    first[j] = first[j] - first[p] * d[j][p]
                left[k + 1] = left[k + 1] - first[p] * r[p]
                right[k + 1] = right[k + 1] - first[p] * q[p]
        for p in range(GROUP):
            at = base + p
            upper_ref[at : at + 1, :] = jnp.where(cols[0:1] >= at, r[p][0:1], 0.0)
            inverse_ref[at : at + 1, :] = q[p][0:1]
        if k + 2 < GROUPS:
            v = [None] * GROUP
            w = [None] * GROUP
            for p in range(GROUP - 1, -1, -1):
                a, b = r[p], q[p]
                for s in range(p + 1, GROUP):
                    a = a - d[s][p] * v[s]
                    b = b - d[s][p] * w[s]
                v[p] = a * inv[p]
                w[p] = b * inv[p]
            for g in range(k + 2, GROUPS):
                mult = c[g - k - 1]
                for p in range(GROUP):
                    left[g] = left[g] - mult[p] * v[p]
                    right[g] = right[g] - mult[p] * w[p]


def remote(src, dst, send, recv, target):
    return pltpu.make_async_remote_copy(
        src_ref=src, dst_ref=dst, send_sem=send, recv_sem=recv, device_id=target, device_id_type=MESH
    )


def panels_kernel(
    a_ref,
    pr_high,
    pr_low,
    pc_high,
    pc_low,
    own,
    flat,
    cbuf,
    rbuf,
    corner,
    upper,
    inverse,
    load_c,
    load_r,
    load_a,
    r_send,
    r_recv,
    k_send,
    k_recv,
    c_send,
    c_recv,
    w_send,
    w_recv,
):
    grid_row = lax.axis_index("row")
    z = lax.axis_index("col")
    core = lax.rem(grid_row, 2)
    y = lax.rem(grid_row // 2, NY)
    x = grid_row // (2 * NY)

    def at(i, j, core_, z_):
        return ((lax.rem(i, NX) * NY + lax.rem(j, NY)) * 2 + core_, lax.rem(z_, NZ))

    sibling = at(x, y, 1 - core, z)
    root = (x == 0) & (y == 0)
    mine = pl.multiple_of(core * BS, BS)

    barrier = pltpu.get_barrier_semaphore()
    near = [at(x + m, y, core, z) for m in range(1, NX)]
    near += [at(x, y + m, core, z) for m in range(1, NY)]
    near += [at(x, y, core, z + m) for m in (1, 2, NZ - 2, NZ - 1)] + [sibling]
    line = [at(x, y, core, z + m) for m in range(3, NZ - 2)]
    for target in near:
        pl.semaphore_signal(barrier, inc=1, device_id=target, device_id_type=MESH)

    @pl.when(root)
    def _():
        for target in line:
            pl.semaphore_signal(barrier, inc=1, device_id=target, device_id_type=MESH)

    def c_load(j):
        return pltpu.make_async_copy(
            a_ref.at[0, :, j, :], cbuf.at[pl.ds(mine, BS), pl.ds(j * BS, BS)], load_c.at[j]
        )

    def r_load(panel, i):
        return pltpu.make_async_copy(a_ref.at[i, :, 0, :], rbuf.at[panel, i], load_r.at[i])

    def a_load(i, j):
        return pltpu.make_async_copy(a_ref.at[i, :, j, :], flat.at[i, :, pl.ds(j * BS, BS)], load_a.at[i, j])

    for panel in range(2):

        @pl.when(z == panel)
        def _():
            for i in range(4):
                r_load(panel, i).start()

    @pl.when(root)
    def _():
        for j in range(16):
            c_load(j).start()

    for panel in range(2):

        @pl.when(z == panel)
        def _():
            for i in range(4):
                r_load(panel, i).wait()

    @pl.when(root)
    def _():
        for j in range(16):
            c_load(j).wait()

    def a_open(i):
        for j in range(16):
            a_load(i, j).start()

    @pl.when(root)
    def _():
        pl.semaphore_wait(barrier, len(near) + len(line))

    @pl.when(jnp.logical_not(root))
    def _():
        pl.semaphore_wait(barrier, len(near))

    def r_copy(panel, i, slot, target):
        view = rbuf.at[panel, i]
        return remote(view, view, r_send.at[panel, i, slot], r_recv.at[panel, i], target)

    def r_sends(panel, i):
        rel = lax.rem(z + NZ - panel, NZ)
        up, up2, down, down2 = [
            r_copy(panel, i, slot, at(x, y, core, z + m)) for slot, m in enumerate((1, 2, NZ - 1, NZ - 2))
        ]
        return [(rel == 0, (up2, down2, up, down)), (rel == 2, (up2, up)), (rel == NZ - 2, (down,))]

    def r_open(panel, i):
        cond, copies = r_sends(panel, i)[0]

        @pl.when(cond)
        def _():
            for copy in copies:
                copy.start()

    def r_relay(i):
        for panel in range(2):
            for cond, copies in r_sends(panel, i)[1:]:

                @pl.when(cond)
                def _(copies=copies):
                    copies[0].wait_recv()
                    for copy in copies:
                        copy.start()

    def r_arrived(panel, i):
        rel = lax.rem(z + NZ - panel, NZ)

        @pl.when((rel != 0) & (rel != 2) & (rel != NZ - 2))
        def _():
            r_copy(panel, i, 0, sibling).wait_recv()

    def r_finish(panel, i):
        for cond, copies in r_sends(panel, i):

            @pl.when(cond)
            def _(copies=copies):
                for copy in copies:
                    copy.wait_send()

    owners = (0, 1, 1)
    planes = (0, 0, 1)

    def k_copy(block, slot, target):
        return remote(corner.at[block], corner.at[block], k_send.at[block, slot], k_recv.at[block], target)

    def k_sends(block):
        owner = core == owners[block]
        source = owner & root & (z == planes[block])
        stages = [(source, [k_copy(block, m - 1, at(x, y, core, z + m)) for m in range(1, NZ)])]
        stages.append((owner, [k_copy(block, NZ - 1, sibling)]))
        return source, stages

    def k_open(block):
        source, stages = k_sends(block)

        @pl.when(source)
        def _():
            corner[block] = rbuf[planes[block], 0]
            for copy in stages[0][1]:
                copy.start()

    def k_relay(block):
        source, stages = k_sends(block)

        @pl.when(jnp.logical_not(source))
        def _():
            k_copy(block, 0, sibling).wait_recv()

        for cond, copies in stages[1:]:

            @pl.when(cond)
            def _(copies=copies):
                for copy in copies:
                    copy.start()

    def k_finish(block):
        for cond, copies in k_sends(block)[1]:

            @pl.when(cond)
            def _(copies=copies):
                for copy in copies:
                    copy.wait_send()

    def c_where(quarter):
        a, b = ((x, y), (y, NX - x), (NX - x, NY - y), (NY - y, x))[quarter]
        place = lax.rem(a, NX) * NY + lax.rem(b, NY)
        depth = jnp.int32(0)
        for (i, j), value in DEPTHS.items():
            depth = jnp.where(place == i * NY + j, value, depth)
        edges = []
        for d in range(4):
            cond = None
            for (i, j), children in CHILDREN.items():
                if d in children:
                    here = place == i * NY + j
                    cond = here if cond is None else cond | here
            if cond is not None:
                step = STEPS[(d + quarter) % 4]
                edges.append((cond, at(x + step[0], y + step[1], core, z)))
        return depth, edges

    c_tree = [c_where(quarter) for quarter in range(QUARTERS)]

    def c_view(quarter, piece, base):
        rows = pl.multiple_of(base + (quarter * (PIECES // 2) + piece // 2) * GROUP, GROUP)
        cols = pl.multiple_of(lax.rem(piece, 2) * (8 * BS), 8 * BS)
        return cbuf.at[pl.ds(rows, GROUP), pl.ds(cols, 8 * BS)]

    def c_copy(quarter, piece, slot, target):
        view = c_view(quarter, piece, mine)
        return remote(view, view, c_send.at[quarter, piece, slot], c_recv.at[quarter, piece, 0], target)

    def c_pair(quarter, piece):
        view = c_view(quarter, piece, mine)
        return remote(view, view, c_send.at[quarter, piece, 4], c_recv.at[quarter, piece, 1], sibling)

    def c_pair_in(quarter, piece):
        view = c_view(quarter, piece, BS - mine)
        return remote(view, view, c_send.at[quarter, piece, 4], c_recv.at[quarter, piece, 1], sibling)

    def c_relay(slot):
        for quarter in range(QUARTERS):
            depth, edges = c_tree[quarter]
            piece = slot - C_LAG * depth

            @pl.when((piece >= 0) & (piece < PIECES))
            def _():
                @pl.when(jnp.logical_not(root))
                def _():
                    c_copy(quarter, piece, 0, sibling).wait_recv()

                for d, (cond, target) in enumerate(edges):

                    @pl.when(cond)
                    def _():
                        c_copy(quarter, piece, d, target).start()

                c_pair(quarter, piece).start()

    def c_finish(quarter, piece):
        for d, (cond, target) in enumerate(c_tree[quarter][1]):

            @pl.when(cond)
            def _():
                c_copy(quarter, piece, d, target).wait_send()

        c_pair(quarter, piece).wait_send()

    half = BS // 2
    a = jnp.where(core == 0, x, y)
    b = jnp.where(core == 0, y, x)

    def w_at(i, j):
        return at(jnp.where(core == 0, i, j), jnp.where(core == 0, j, i), core, z)

    def w_view(part):
        rows = pl.ds(pl.multiple_of(core * half, half), half)
        return inverse.at[pl.ds(0, 1) if part == 0 else pl.ds(1, 2), rows]

    def w_copy(part, slot, target):
        return remote(w_view(part), w_view(part), w_send.at[part, slot], w_recv.at[part, 0], target)

    def w_pair(part):
        return remote(w_view(part), w_view(part), w_send.at[part, 6], w_recv.at[part, 1], sibling)

    def w_sends(part):
        return [
            (root, [w_copy(part, m - 1, w_at(a + m, b)) for m in range(1, NX)]),
            (b == 0, [w_copy(part, 2 + m, w_at(a, b + m)) for m in range(1, NY)]),
            (jnp.logical_not(root), [w_pair(part)]),
        ]

    def w_relay(part):
        @pl.when(jnp.logical_not(root))
        def _():
            w_copy(part, 0, sibling).wait_recv()

        for cond, copies in w_sends(part):

            @pl.when(cond)
            def _(copies=copies):
                for copy in copies:
                    copy.start()

    def w_arrived(part):
        @pl.when(jnp.logical_not(root))
        def _():
            w_pair(part).wait_recv()

    def w_finish(part):
        for cond, copies in w_sends(part):

            @pl.when(cond)
            def _(copies=copies):
                for copy in copies:
                    copy.wait_send()

    last_c = PIECES + DEEPEST * C_LAG

    @pl.when(root)
    def _():
        k_open(0)
        k_open(1)
        k_open(2)
        c_relay(0)
        for i in range(4):
            for panel in range(2):
                r_open(panel, i)
            c_relay(1 + i)
        k_relay(0)
        todo = {(0, 1 + i): (c_relay, 5 + i) for i in range(3)}
        todo |= {(0, 6): (k_relay, 1), (0, 8): (k_relay, 2), (1, 4): (r_relay, 0)}
        todo |= {(1, 2): (a_open, 0), (1, 6): (a_open, 1), (1, 10): (a_open, 2), (1, 14): (a_open, 3)}

        def hook(panel):
            def run(k):
                if (panel, k) in todo:
                    f, value = todo[panel, k]
                    f(value)

            return run

        factor_block(corner[0], upper.at[0], inverse.at[0], hook(0))
        w_relay(0)
        below = dot_nt(corner[1], inverse[0])
        second = corner[2] - dot_nt(below, below)
        through = dot_nn(below, inverse[0])
        factor_block(second, upper.at[1], inverse.at[2], hook(1))
        inverse[1] = -dot_nn(inverse[2], through)
        w_relay(1)
        for i in range(1, 4):
            r_relay(i)

    @pl.when(jnp.logical_not(root))
    def _():
        for i in range(4):
            for panel in range(2):
                r_open(panel, i)
        relays = {6: 0, 11: 1, 16: 2, 21: 3}
        for slot in range(last_c):
            c_relay(slot)
            if 1 <= slot <= 4:
                a_open(slot - 1)
            if slot in relays:
                r_relay(relays[slot])
            if slot == last_c - 5:
                w_relay(0)
        w_relay(1)

    for panel in range(2):
        for i in range(4):
            r_arrived(panel, i)
    for part in range(2):
        w_arrived(part)

    zero = jnp.zeros((BS, BS), jnp.float32)
    top = jnp.concatenate([inverse[0], zero], 1)
    whole = split(jnp.concatenate([top, jnp.concatenate([inverse[1], inverse[2]], 1)], 0))
    for i in range(4):
        rows = dot3(split(jnp.concatenate([rbuf[0, i], rbuf[1, i]], 1)), whole, 1)
        pr_high[i], pr_low[i] = split(dot3(split(rows), whole, 0))
        for panel in range(2):

            @pl.when(z == panel)
            def _():
                own[i] = rows[:, panel * BS : (panel + 1) * BS]

    @pl.when((grid_row == 0) & (z == 0))
    def _():
        own[0] = upper[0].T

    @pl.when((grid_row == 0) & (z == 1))
    def _():
        own[0] = jnp.zeros((BS, BS), jnp.float32)

    @pl.when((grid_row == 1) & (z == 1))
    def _():
        own[0] = upper[1].T

    for quarter in range(QUARTERS):
        for piece in range(PIECES):
            c_pair_in(quarter, piece).wait_recv()
    pc_high[...], pc_low[...] = split(cbuf[...])

    for part in range(2):
        w_finish(part)
    for i in range(4):
        for panel in range(2):
            r_finish(panel, i)

    @pl.when(root)
    def _():
        for block in range(3):
            k_finish(block)

    for quarter in range(QUARTERS):
        for piece in range(PIECES):
            c_finish(quarter, piece)
    for i in range(4):
        for j in range(16):
            a_load(i, j).wait()


def update_kernel(flat, pr_high, pr_low, pc_high, pc_low, own, out_ref, tiles, store):
    grid_row = lax.axis_index("row")
    z = lax.axis_index("col")
    wide = 4

    def out_copy(i):
        return pltpu.make_async_copy(tiles.at[i], out_ref.at[i], store.at[i])

    for i in range(4):
        for j in range(0, 16, wide):
            part = slice(j * BS, (j + wide) * BS)
            rows = (pr_high[i], pr_low[i])
            new = flat[i, :, part] - dot3(rows, (pc_high[:, part], pc_low[:, part]), 0)
            for m in range(wide):
                tiles[i, :, j + m, :] = new[:, m * BS : (m + 1) * BS]
        if i == 0:

            @pl.when(grid_row < 2)
            def _():
                tiles[0] = jnp.zeros((BS, 16, BS), jnp.float32)

        @pl.when(z < 2)
        def _():
            tiles[i, :, 0, :] = own[i]

        out_copy(i).start()
    for i in range(4):
        out_copy(i).wait()


def shards(kernel):
    f32, bf16 = jnp.float32, jnp.bfloat16
    vmem = pl.BlockSpec(memory_space=pltpu.VMEM)
    *factors, flat = pl.pallas_call(
        panels_kernel,
        out_shape=[
            jax.ShapeDtypeStruct((4, BS, 2 * BS), bf16),
            jax.ShapeDtypeStruct((4, BS, 2 * BS), bf16),
            jax.ShapeDtypeStruct((2 * BS, 16 * BS), bf16),
            jax.ShapeDtypeStruct((2 * BS, 16 * BS), bf16),
            jax.ShapeDtypeStruct((4, BS, BS), f32),
            jax.ShapeDtypeStruct((4, BS, 16 * BS), f32),
        ],
        in_specs=[pl.BlockSpec(memory_space=pltpu.HBM)],
        out_specs=[vmem] * 6,
        scratch_shapes=[
            pltpu.VMEM((2 * BS, 16 * BS), f32),
            pltpu.VMEM((2, 4, BS, BS), f32),
            pltpu.VMEM((3, BS, BS), f32),
            pltpu.VMEM((2, BS, BS), f32),
            pltpu.VMEM((3, BS, BS), f32),
            pltpu.SemaphoreType.DMA((16,)),
            pltpu.SemaphoreType.DMA((4,)),
            pltpu.SemaphoreType.DMA((4, 16)),
            pltpu.SemaphoreType.DMA((2, 4, 4)),
            pltpu.SemaphoreType.DMA((2, 4)),
            pltpu.SemaphoreType.DMA((3, NZ)),
            pltpu.SemaphoreType.DMA((3,)),
            pltpu.SemaphoreType.DMA((QUARTERS, PIECES, 5)),
            pltpu.SemaphoreType.DMA((QUARTERS, PIECES, 2)),
            pltpu.SemaphoreType.DMA((2, 7)),
            pltpu.SemaphoreType.DMA((2, 2)),
        ],
        compiler_params=pltpu.CompilerParams(
            collective_id=0, has_side_effects=True, vmem_limit_bytes=44 * 1024 * 1024
        ),
        name="panels",
    )(kernel)
    return pl.pallas_call(
        update_kernel,
        out_shape=jax.ShapeDtypeStruct(kernel.shape, f32),
        in_specs=[vmem] * 6,
        out_specs=pl.BlockSpec(memory_space=pltpu.HBM),
        scratch_shapes=[pltpu.VMEM((4, BS, 16, BS), f32), pltpu.SemaphoreType.DMA((4,))],
        compiler_params=pltpu.CompilerParams(vmem_limit_bytes=32 * 1024 * 1024),
        name="update",
    )(flat, *factors)


def solution(mesh):
    spec = P(None, "row", None, "col")
    return jax.shard_map(shards, mesh=mesh, in_specs=(spec,), out_specs=spec, check_vma=False)
```

```python
import jax
import jax.numpy as jnp
from jax import lax
from jax.experimental import pallas as pl
from jax.experimental.pallas import tpu as pltpu
from jax.sharding import PartitionSpec as P

NX, NY, NZ = 4, 4, 8
BS = 128
GROUP = 8
GROUPS = BS // GROUP
QUARTERS = 4
PIECES = 8
C_LAG = 4
STEPS = ((1, 0), (0, 1), (NX - 1, 0), (0, NY - 1))
CHILDREN = {
    (0, 0): (0,),
    (1, 0): (0, 1, 3),
    (2, 0): (3, 0),
    (1, 1): (1, 2, 0),
    (1, 3): (2,),
    (2, 1): (0,),
    (2, 3): (3, 0),
    (1, 2): (2,),
    (2, 2): (0,),
}


def tree_depths():
    depths = {(0, 0): 0}
    todo = [(0, 0)]
    while todo:
        a, b = todo.pop()
        for d in CHILDREN.get((a, b), ()):
            child = ((a + STEPS[d][0]) % NX, (b + STEPS[d][1]) % NY)
            depths[child] = depths[(a, b)] + 1
            todo.append(child)
    return depths


DEPTHS = tree_depths()
assert len(DEPTHS) == NX * NY
DEEPEST = max(DEPTHS.values())
MESH = pl.DeviceIdType.MESH


def dot_nn(a, b):
    return lax.dot_general(
        a,
        b,
        (((1,), (0,)), ((), ())),
        precision=lax.Precision.HIGHEST,
        preferred_element_type=jnp.float32,
    )


def dot_nt(a, b):
    return lax.dot_general(
        a,
        b,
        (((1,), (1,)), ((), ())),
        precision=lax.Precision.HIGHEST,
        preferred_element_type=jnp.float32,
    )


def split(value):
    high = value.astype(jnp.bfloat16)
    return high, (value - high.astype(jnp.float32)).astype(jnp.bfloat16)


def dot3(a, b, over):
    def one(p, q):
        return lax.dot_general(p, q, (((1,), (over,)), ((), ())), preferred_element_type=jnp.float32)

    return one(a[0], b[0]) + (one(a[1], b[0]) + one(a[0], b[1]))


def lane(value, index):
    return jnp.broadcast_to(value[:, index : index + 1], (GROUP, BS))


def factor_block(block, upper_ref, inverse_ref, hook):
    rows = lax.broadcasted_iota(jnp.int32, (GROUP, BS), 0)
    cols = lax.broadcasted_iota(jnp.int32, (GROUP, BS), 1)
    left = [block[GROUP * g : GROUP * (g + 1), :] for g in range(GROUPS)]
    right = [jnp.where(cols == rows + GROUP * g, 1.0, 0.0).astype(jnp.float32) for g in range(GROUPS)]
    for k in range(GROUPS):
        hook(k)
        base = GROUP * k
        r = [jnp.broadcast_to(left[k][i : i + 1, :], (GROUP, BS)) for i in range(GROUP)]
        q = [jnp.broadcast_to(right[k][i : i + 1, :], (GROUP, BS)) for i in range(GROUP)]
        d = [[lane(r[i], base + j) if j <= i else None for j in range(GROUP)] for i in range(GROUP)]
        c = [[lane(left[g], base + p) for p in range(GROUP)] for g in range(k + 1, GROUPS)]
        inv = [None] * GROUP
        for p in range(GROUP):
            inv[p] = lax.rsqrt(d[p][p])
            for i in range(p + 1, GROUP):
                d[i][p] = d[i][p] * inv[p]
            r[p] = r[p] * inv[p]
            q[p] = q[p] * inv[p]
            for i in range(p + 1, GROUP):
                for j in range(p + 1, i + 1):
                    d[i][j] = d[i][j] - d[i][p] * d[j][p]
                r[i] = r[i] - d[i][p] * r[p]
                q[i] = q[i] - d[i][p] * q[p]
            if k + 1 < GROUPS:
                first = c[0]
                first[p] = first[p] * inv[p]
                for j in range(p + 1, GROUP):
                    first[j] = first[j] - first[p] * d[j][p]
                left[k + 1] = left[k + 1] - first[p] * r[p]
                right[k + 1] = right[k + 1] - first[p] * q[p]
        for p in range(GROUP):
            at = base + p
            upper_ref[at : at + 1, :] = jnp.where(cols[0:1] >= at, r[p][0:1], 0.0)
            inverse_ref[at : at + 1, :] = q[p][0:1]
        if k + 2 < GROUPS:
            v = [None] * GROUP
            w = [None] * GROUP
            for p in range(GROUP - 1, -1, -1):
                a, b = r[p], q[p]
                for s in range(p + 1, GROUP):
                    a = a - d[s][p] * v[s]
                    b = b - d[s][p] * w[s]
                v[p] = a * inv[p]
                w[p] = b * inv[p]
            for g in range(k + 2, GROUPS):
                mult = c[g - k - 1]
                for p in range(GROUP):
                    left[g] = left[g] - mult[p] * v[p]
                    right[g] = right[g] - mult[p] * w[p]


def remote(src, dst, send, recv, target):
    return pltpu.make_async_remote_copy(
        src_ref=src, dst_ref=dst, send_sem=send, recv_sem=recv, device_id=target, device_id_type=MESH
    )


def panels_kernel(
    a_ref,
    pr_high,
    pr_low,
    pc_high,
    pc_low,
    own,
    flat,
    cbuf,
    rbuf,
    corner,
    upper,
    inverse,
    load_c,
    load_r,
    load_a,
    r_send,
    r_recv,
    k_send,
    k_recv,
    c_send,
    c_recv,
    w_send,
    w_recv,
):
    grid_row = lax.axis_index("row")
    z = lax.axis_index("col")
    core = lax.rem(grid_row, 2)
    y = lax.rem(grid_row // 2, NY)
    x = grid_row // (2 * NY)

    def at(i, j, core_, z_):
        return ((lax.rem(i, NX) * NY + lax.rem(j, NY)) * 2 + core_, lax.rem(z_, NZ))

    sibling = at(x, y, 1 - core, z)
    root = (x == 0) & (y == 0)
    mine = pl.multiple_of(core * BS, BS)

    barrier = pltpu.get_barrier_semaphore()
    near = [at(x + m, y, core, z) for m in range(1, NX)]
    near += [at(x, y + m, core, z) for m in range(1, NY)]
    near += [at(x, y, core, z + m) for m in (1, 2, NZ - 2, NZ - 1)] + [sibling]
    line = [at(x, y, core, z + m) for m in range(3, NZ - 2)]
    for target in near:
        pl.semaphore_signal(barrier, inc=1, device_id=target, device_id_type=MESH)

    @pl.when(root)
    def _():
        for target in line:
            pl.semaphore_signal(barrier, inc=1, device_id=target, device_id_type=MESH)

    def c_load(j):
        return pltpu.make_async_copy(
            a_ref.at[0, :, j, :], cbuf.at[pl.ds(mine, BS), pl.ds(j * BS, BS)], load_c.at[j]
        )

    def r_load(panel, i):
        return pltpu.make_async_copy(a_ref.at[i, :, 0, :], rbuf.at[panel, i], load_r.at[i])

    def a_load(i, j):
        return pltpu.make_async_copy(a_ref.at[i, :, j, :], flat.at[i, :, pl.ds(j * BS, BS)], load_a.at[i, j])

    for panel in range(2):

        @pl.when(z == panel)
        def _():
            for i in range(4):
                r_load(panel, i).start()

    @pl.when(root)
    def _():
        for j in range(16):
            c_load(j).start()

    for panel in range(2):

        @pl.when(z == panel)
        def _():
            for i in range(4):
                r_load(panel, i).wait()

    @pl.when(root)
    def _():
        for j in range(16):
            c_load(j).wait()

    def a_open(i):
        for j in range(16):
            a_load(i, j).start()

    @pl.when(root)
    def _():
        pl.semaphore_wait(barrier, len(near) + len(line))

    @pl.when(jnp.logical_not(root))
    def _():
        pl.semaphore_wait(barrier, len(near))

    def r_copy(panel, i, slot, target):
        view = rbuf.at[panel, i]
        return remote(view, view, r_send.at[panel, i, slot], r_recv.at[panel, i], target)

    def r_sends(panel, i):
        rel = lax.rem(z + NZ - panel, NZ)
        up, up2, down, down2 = [
            r_copy(panel, i, slot, at(x, y, core, z + m)) for slot, m in enumerate((1, 2, NZ - 1, NZ - 2))
        ]
        return [(rel == 0, (up2, down2, up, down)), (rel == 2, (up2, up)), (rel == NZ - 2, (down,))]

    def r_open(panel, i):
        cond, copies = r_sends(panel, i)[0]

        @pl.when(cond)
        def _():
            for copy in copies:
                copy.start()

    def r_relay(i):
        for panel in range(2):
            for cond, copies in r_sends(panel, i)[1:]:

                @pl.when(cond)
                def _(copies=copies):
                    copies[0].wait_recv()
                    for copy in copies:
                        copy.start()

    def r_arrived(panel, i):
        rel = lax.rem(z + NZ - panel, NZ)

        @pl.when((rel != 0) & (rel != 2) & (rel != NZ - 2))
        def _():
            r_copy(panel, i, 0, sibling).wait_recv()

    def r_finish(panel, i):
        for cond, copies in r_sends(panel, i):

            @pl.when(cond)
            def _(copies=copies):
                for copy in copies:
                    copy.wait_send()

    owners = (0, 1, 1)
    planes = (0, 0, 1)

    def k_copy(block, slot, target):
        return remote(corner.at[block], corner.at[block], k_send.at[block, slot], k_recv.at[block], target)

    def k_sends(block):
        owner = core == owners[block]
        source = owner & root & (z == planes[block])
        stages = [(source, [k_copy(block, m - 1, at(x, y, core, z + m)) for m in range(1, NZ)])]
        stages.append((owner, [k_copy(block, NZ - 1, sibling)]))
        return source, stages

    def k_open(block):
        source, stages = k_sends(block)

        @pl.when(source)
        def _():
            corner[block] = rbuf[planes[block], 0]
            for copy in stages[0][1]:
                copy.start()

    def k_relay(block):
        source, stages = k_sends(block)

        @pl.when(jnp.logical_not(source))
        def _():
            k_copy(block, 0, sibling).wait_recv()

        for cond, copies in stages[1:]:

            @pl.when(cond)
            def _(copies=copies):
                for copy in copies:
                    copy.start()

    def k_finish(block):
        for cond, copies in k_sends(block)[1]:

            @pl.when(cond)
            def _(copies=copies):
                for copy in copies:
                    copy.wait_send()

    def c_where(quarter):
        a, b = ((x, y), (y, NX - x), (NX - x, NY - y), (NY - y, x))[quarter]
        place = lax.rem(a, NX) * NY + lax.rem(b, NY)
        depth = jnp.int32(0)
        for (i, j), value in DEPTHS.items():
            depth = jnp.where(place == i * NY + j, value, depth)
        edges = []
        for d in range(4):
            cond = None
            for (i, j), children in CHILDREN.items():
                if d in children:
                    here = place == i * NY + j
                    cond = here if cond is None else cond | here
            if cond is not None:
                step = STEPS[(d + quarter) % 4]
                edges.append((cond, at(x + step[0], y + step[1], core, z)))
        return depth, edges

    c_tree = [c_where(quarter) for quarter in range(QUARTERS)]

    def c_view(quarter, piece, base):
        rows = pl.multiple_of(base + (quarter * (PIECES // 2) + piece // 2) * GROUP, GROUP)
        cols = pl.multiple_of(lax.rem(piece, 2) * (8 * BS), 8 * BS)
        return cbuf.at[pl.ds(rows, GROUP), pl.ds(cols, 8 * BS)]

    def c_copy(quarter, piece, slot, target):
        view = c_view(quarter, piece, mine)
        return remote(view, view, c_send.at[quarter, piece, slot], c_recv.at[quarter, piece, 0], target)

    def c_pair(quarter, piece):
        view = c_view(quarter, piece, mine)
        return remote(view, view, c_send.at[quarter, piece, 4], c_recv.at[quarter, piece, 1], sibling)

    def c_pair_in(quarter, piece):
        view = c_view(quarter, piece, BS - mine)
        return remote(view, view, c_send.at[quarter, piece, 4], c_recv.at[quarter, piece, 1], sibling)

    def c_relay(slot):
        for quarter in range(QUARTERS):
            depth, edges = c_tree[quarter]
            piece = slot - C_LAG * depth

            @pl.when((piece >= 0) & (piece < PIECES))
            def _():
                @pl.when(jnp.logical_not(root))
                def _():
                    c_copy(quarter, piece, 0, sibling).wait_recv()

                for d, (cond, target) in enumerate(edges):

                    @pl.when(cond)
                    def _():
                        c_copy(quarter, piece, d, target).start()

                c_pair(quarter, piece).start()

    def c_finish(quarter, piece):
        for d, (cond, target) in enumerate(c_tree[quarter][1]):

            @pl.when(cond)
            def _():
                c_copy(quarter, piece, d, target).wait_send()

        c_pair(quarter, piece).wait_send()

    half = BS // 2
    a = jnp.where(core == 0, x, y)
    b = jnp.where(core == 0, y, x)

    def w_at(i, j):
        return at(jnp.where(core == 0, i, j), jnp.where(core == 0, j, i), core, z)

    def w_view(part):
        rows = pl.ds(pl.multiple_of(core * half, half), half)
        return inverse.at[pl.ds(0, 1) if part == 0 else pl.ds(1, 2), rows]

    def w_copy(part, slot, target):
        return remote(w_view(part), w_view(part), w_send.at[part, slot], w_recv.at[part, 0], target)

    def w_pair(part):
        return remote(w_view(part), w_view(part), w_send.at[part, 6], w_recv.at[part, 1], sibling)

    def w_sends(part):
        return [
            (root, [w_copy(part, m - 1, w_at(a + m, b)) for m in range(1, NX)]),
            (b == 0, [w_copy(part, 2 + m, w_at(a, b + m)) for m in range(1, NY)]),
            (jnp.logical_not(root), [w_pair(part)]),
        ]

    def w_relay(part):
        @pl.when(jnp.logical_not(root))
        def _():
            w_copy(part, 0, sibling).wait_recv()

        for cond, copies in w_sends(part):

            @pl.when(cond)
            def _(copies=copies):
                for copy in copies:
                    copy.start()

    def w_arrived(part):
        @pl.when(jnp.logical_not(root))
        def _():
            w_pair(part).wait_recv()

    def w_finish(part):
        for cond, copies in w_sends(part):

            @pl.when(cond)
            def _(copies=copies):
                for copy in copies:
                    copy.wait_send()

    last_c = PIECES + DEEPEST * C_LAG

    @pl.when(root)
    def _():
        k_open(0)
        k_open(1)
        k_open(2)
        c_relay(0)
        for i in range(4):
            for panel in range(2):
                r_open(panel, i)
            c_relay(1 + i)
        k_relay(0)
        todo = {(0, 1 + i): (c_relay, 5 + i) for i in range(3)}
        todo |= {(0, 6): (k_relay, 1), (0, 8): (k_relay, 2), (1, 4): (r_relay, 0), (1, 12): (r_relay, 1)}
        todo |= {(1, 2): (a_open, 0), (1, 6): (a_open, 1), (1, 10): (a_open, 2), (1, 14): (a_open, 3)}

        def hook(panel):
            def run(k):
                if (panel, k) in todo:
                    f, value = todo[panel, k]
                    f(value)

            return run

        factor_block(corner[0], upper.at[0], inverse.at[0], hook(0))
        w_relay(0)
        below = dot_nt(corner[1], inverse[0])
        second = corner[2] - dot_nt(below, below)
        through = dot_nn(below, inverse[0])
        factor_block(second, upper.at[1], inverse.at[2], hook(1))
        inverse[1] = -dot_nn(inverse[2], through)
        w_relay(1)
        for i in range(2, 4):
            r_relay(i)

    @pl.when(jnp.logical_not(root))
    def _():
        for i in range(4):
            for panel in range(2):
                r_open(panel, i)
        relays = {6: 0, 11: 1, 16: 2, 21: 3}
        for slot in range(last_c):
            c_relay(slot)
            if 1 <= slot <= 4:
                a_open(slot - 1)
            if slot in relays:
                r_relay(relays[slot])
            if slot == last_c - 5:
                w_relay(0)
        w_relay(1)

    for panel in range(2):
        for i in range(4):
            r_arrived(panel, i)
    for part in range(2):
        w_arrived(part)

    zero = jnp.zeros((BS, BS), jnp.float32)
    top = jnp.concatenate([inverse[0], zero], 1)
    whole = split(jnp.concatenate([top, jnp.concatenate([inverse[1], inverse[2]], 1)], 0))
    for i in range(4):
        rows = dot3(split(jnp.concatenate([rbuf[0, i], rbuf[1, i]], 1)), whole, 1)
        pr_high[i], pr_low[i] = split(dot3(split(rows), whole, 0))
        for panel in range(2):

            @pl.when(z == panel)
            def _():
                own[i] = rows[:, panel * BS : (panel + 1) * BS]

    @pl.when((grid_row == 0) & (z == 0))
    def _():
        own[0] = upper[0].T

    @pl.when((grid_row == 0) & (z == 1))
    def _():
        own[0] = jnp.zeros((BS, BS), jnp.float32)

    @pl.when((grid_row == 1) & (z == 1))
    def _():
        own[0] = upper[1].T

    for quarter in range(QUARTERS):
        for piece in range(PIECES):
            c_pair_in(quarter, piece).wait_recv()
    pc_high[...], pc_low[...] = split(cbuf[...])

    for part in range(2):
        w_finish(part)
    for i in range(4):
        for panel in range(2):
            r_finish(panel, i)

    @pl.when(root)
    def _():
        for block in range(3):
            k_finish(block)

    for quarter in range(QUARTERS):
        for piece in range(PIECES):
            c_finish(quarter, piece)
    for i in range(4):
        for j in range(16):
            a_load(i, j).wait()


def update_kernel(flat, pr_high, pr_low, pc_high, pc_low, own, out_ref, tiles, store):
    grid_row = lax.axis_index("row")
    z = lax.axis_index("col")
    wide = 4

    def out_copy(i):
        return pltpu.make_async_copy(tiles.at[i], out_ref.at[i], store.at[i])

    for i in range(4):
        for j in range(0, 16, wide):
            part = slice(j * BS, (j + wide) * BS)
            rows = (pr_high[i], pr_low[i])
            new = flat[i, :, part] - dot3(rows, (pc_high[:, part], pc_low[:, part]), 0)
            for m in range(wide):
                tiles[i, :, j + m, :] = new[:, m * BS : (m + 1) * BS]
        if i == 0:

            @pl.when(grid_row < 2)
            def _():
                tiles[0] = jnp.zeros((BS, 16, BS), jnp.float32)

        @pl.when(z < 2)
        def _():
            tiles[i, :, 0, :] = own[i]

        out_copy(i).start()
    for i in range(4):
        out_copy(i).wait()


def shards(kernel):
    f32, bf16 = jnp.float32, jnp.bfloat16
    vmem = pl.BlockSpec(memory_space=pltpu.VMEM)
    *factors, flat = pl.pallas_call(
        panels_kernel,
        out_shape=[
            jax.ShapeDtypeStruct((4, BS, 2 * BS), bf16),
            jax.ShapeDtypeStruct((4, BS, 2 * BS), bf16),
            jax.ShapeDtypeStruct((2 * BS, 16 * BS), bf16),
            jax.ShapeDtypeStruct((2 * BS, 16 * BS), bf16),
            jax.ShapeDtypeStruct((4, BS, BS), f32),
            jax.ShapeDtypeStruct((4, BS, 16 * BS), f32),
        ],
        in_specs=[pl.BlockSpec(memory_space=pltpu.HBM)],
        out_specs=[vmem] * 6,
        scratch_shapes=[
            pltpu.VMEM((2 * BS, 16 * BS), f32),
            pltpu.VMEM((2, 4, BS, BS), f32),
            pltpu.VMEM((3, BS, BS), f32),
            pltpu.VMEM((2, BS, BS), f32),
            pltpu.VMEM((3, BS, BS), f32),
            pltpu.SemaphoreType.DMA((16,)),
            pltpu.SemaphoreType.DMA((4,)),
            pltpu.SemaphoreType.DMA((4, 16)),
            pltpu.SemaphoreType.DMA((2, 4, 4)),
            pltpu.SemaphoreType.DMA((2, 4)),
            pltpu.SemaphoreType.DMA((3, NZ)),
            pltpu.SemaphoreType.DMA((3,)),
            pltpu.SemaphoreType.DMA((QUARTERS, PIECES, 5)),
            pltpu.SemaphoreType.DMA((QUARTERS, PIECES, 2)),
            pltpu.SemaphoreType.DMA((2, 7)),
            pltpu.SemaphoreType.DMA((2, 2)),
        ],
        compiler_params=pltpu.CompilerParams(
            collective_id=0, has_side_effects=True, vmem_limit_bytes=44 * 1024 * 1024
        ),
        name="panels",
    )(kernel)
    return pl.pallas_call(
        update_kernel,
        out_shape=jax.ShapeDtypeStruct(kernel.shape, f32),
        in_specs=[vmem] * 6,
        out_specs=pl.BlockSpec(memory_space=pltpu.HBM),
        scratch_shapes=[pltpu.VMEM((4, BS, 16, BS), f32), pltpu.SemaphoreType.DMA((4,))],
        compiler_params=pltpu.CompilerParams(vmem_limit_bytes=32 * 1024 * 1024),
        name="update",
    )(flat, *factors)


def solution(mesh):
    spec = P(None, "row", None, "col")
    return jax.shard_map(shards, mesh=mesh, in_specs=(spec,), out_specs=spec, check_vma=False)
```
